32 devices in a mesh: dp: 8 (over z, x), expert: 4 (over y, core).
Axes of the slice: x: 2, y: 2, z: 4, core: 2. Of those that a mesh axis runs over, the one named last changes fastest.
Arguments:
- tokens: float32 [4096, 1664], P('dp'), may hold values from -6 to 6
- ln_gain: float32 [1664], replicated, may hold values from 0.1 to 1.9
- ln_bias: float32 [1664], replicated, may hold values from -3 to 3
- weight_in: bfloat16 [16, 1664, 8192], P('dp', None, 'expert'), may hold values from -0.15625 to 0.15625
- weight_out: bfloat16 [16, 8192, 1664], P('dp', 'expert'), may hold values from -0.0625 to 0.0625
- expert_ids: int32 [4096, 2], P('dp'), may hold values from 0 to 15, all different within a row; in each aligned block of 512 rows (0 to 511, 512 to 1023, ...) at most 80 rows name the same one
- combine_weights: float32 [4096, 2], P('dp'), may hold values from 0.2 to 1
- owner_ids: int32 [16, 1], replicated, may hold values from 0 to 7; in each aligned block of 16 rows (0 to 15, 16 to 31, ...) at most 4 rows name the same one
Outputs:
- delivered: float32 [8192, 1664], P('dp', 'expert')
The draws below stay inside these ranges and needn't reach their ends.
Inputs may be any that keep to these rules, and one draw needn't show every extreme that they name: `expert_ids`: the two entries of a row differ. In each aligned block of 512 rows no expert is named more than 80 times. `owner_ids`: no owner is named more than 4 times.
All inputs are finite; a program needn't handle non-finite values.
Results may differ from the reference program's by a relative error of at most 0.008.
Values may be sent and summed in bfloat16 or wider, within the bound.
No kernel may reach another device: no remote copies, remote signals or barrier semaphores. Data moves between devices by JAX's collectives and lax.ppermute only.
A program may use at most 128 MiB of HBM per device.

```python
import math
import jax
import jax.numpy as jnp
import numpy as np
from jax import lax

D = 1664
FF = 8192
PATCH = 256
TOK_DEV = 512
CAP = 80
OWN_IMG = 4
EXPERTS = 16
TOKENS = 4096
IMAGES = 16
N_DP = 8
N_EXPERT = 4


def block_scale(key, dims, cuts, least, high):
    def one(position, blocks):
        steps = jax.random.uniform(jax.random.fold_in(jax.random.fold_in(key, 6), position), (blocks,), jnp.float32, least / len(cuts), high / len(cuts))
        return jnp.repeat(jnp.exp(steps), dims[position] // blocks).reshape((-1,) + (1,) * (len(dims) - position - 1))

    gain = one(*cuts[0])
    for cut in cuts[1:]:
        gain = gain * one(*cut)
    return gain


def assign_block(own_key, own, number, rows, count, top, reach, slope):
    ranking = jax.random.permutation(own_key, count)
    packed, common = shares(count, rows * top, reach, slope, True), shares(count, rows * top, reach, slope, False)
    places = jnp.arange(count)

    def named(lengths, rotation):
        used = int((lengths > 0).sum())
        fixed = max(1, used // 4)
        passed = fixed + (places - fixed + rotation * (used - fixed)) % max(1, count - fixed)
        return jnp.zeros((count,), jnp.int32).at[ranking[jnp.where(places < fixed, places, passed)]].set(jnp.asarray(lengths, jnp.int32))

    lengths = jnp.where(number % 4 == 0, named(packed, number // 4), named(common, number - number // 4 - 1))
    mixed = jax.random.permutation(jax.random.fold_in(own, 3), count)
    source_of, receiver = mixed[0:count // 2 * 2:2], mixed[1:count // 2 * 2:2]
    room = jnp.minimum(lengths[source_of] - 1, reach - lengths[receiver]) // 2
    room = jnp.where((source_of == ranking[0]) | (receiver == ranking[0]) | (lengths[receiver] == 0), 0, jnp.maximum(room, 0))
    passed = jax.random.randint(jax.random.fold_in(own, 4), (count // 2,), 0, 1 << 20) % (room + 1)
    lengths = lengths.at[source_of].add(-passed).at[receiver].add(passed)
    members = jnp.searchsorted(jnp.cumsum(lengths), jnp.arange(rows * top), side="right").astype(jnp.int32)
    listing = members.reshape(top, rows).T
    listing = listing[jax.random.permutation(jax.random.fold_in(own, 1), rows)]
    rotation = jax.random.randint(jax.random.fold_in(own, 2), (rows, 1), 0, top)
    return jnp.take_along_axis(listing, (jnp.arange(top)[None, :] + rotation) % top, axis=1)


def shares(count, total, reach, slope, full):
    portions = [(1 << 20) // math.isqrt(grade ** slope) + 1 for grade in range(1, count + 1)]
    largest = reach if full else min(reach, max(-(-total // count), total * portions[0] // sum(portions)))
    least = 1 if total - largest >= count - 1 else 0
    counts, surplus = [largest] + [least] * (count - 1), total - largest - least * (count - 1)
    while surplus > 0:
        movable = [i for i in range(1, count) if counts[i] < largest] or [i for i in range(1, count) if counts[i] < reach]
        mass, remaining = sum([portions[i] for i in movable]), surplus
        for i in movable:
            extra = min(reach - counts[i], max(1, remaining * portions[i] // mass), surplus)
            counts[i] = counts[i] + extra
            surplus = surplus - extra
    return np.array(counts)


def noise(key, dims, width, reach, pieces=(), held_as=jnp.bfloat16):
    drawn = width * jax.random.normal(key, dims, jnp.float32)
    if pieces:
        drawn = drawn * block_scale(key, dims, pieces, -0.22, 0.18)
    return jnp.clip(drawn, -reach, reach).astype(held_as)


def setup_inputs(seed: int = 0) -> dict:
    keys = jax.random.split(jax.random.key(seed), 9)
    tokens = noise(keys[0], (TOKENS, D), 1.0, 6.0, ((0, 8),), jnp.float32)
    ln_gain = jnp.clip(1.0 + 0.18 * jax.random.normal(keys[1], (D,), jnp.float32), 0.1, 1.9)
    ln_bias = noise(keys[2], (D,), 0.5, 3.0, (), jnp.float32)
    weight_in = noise(keys[3], (EXPERTS, D, FF), D ** -0.5, 0.15625, ((0, 8), (2, 4)))
    weight_out = noise(keys[4], (EXPERTS, FF, D), FF ** -0.5, 0.0625, ((0, 8), (1, 4)))
    expert_ids_keys = jax.random.split(jax.random.fold_in(keys[5], 1), TOKENS // TOK_DEV)
    expert_ids_turns = jax.random.permutation(jax.random.fold_in(keys[5], 3), TOKENS // TOK_DEV)
    expert_ids = jax.vmap(lambda own, number: assign_block(jax.random.fold_in(keys[5], 2), own, number, TOK_DEV, EXPERTS, 2, CAP, 2))(expert_ids_keys, expert_ids_turns).reshape((TOKENS, 2))
    combine_weights = jnp.clip(0.2 + 0.8 * jax.random.uniform(keys[6], (TOKENS, 2), jnp.float32) ** block_scale(keys[6], (TOKENS, 2), ((0, 8),), -0.2, 0.2), 0.2, 1.0)
    owner_ids_keys = jax.random.split(jax.random.fold_in(keys[7], 1), IMAGES // IMAGES)
    owner_ids_turns = jax.random.permutation(jax.random.fold_in(keys[7], 3), IMAGES // IMAGES)
    owner_ids = jax.vmap(lambda own, number: assign_block(jax.random.fold_in(keys[7], 2), own, number, IMAGES, N_DP, 1, OWN_IMG, 2))(owner_ids_keys, owner_ids_turns).reshape((IMAGES, 1))
    return {"tokens": tokens, "ln_gain": ln_gain, "ln_bias": ln_bias, "weight_in": weight_in, "weight_out": weight_out, "expert_ids": expert_ids, "combine_weights": combine_weights, "owner_ids": owner_ids}


epsilon = 1e-06

def normalize(tokens, ln_gain, ln_bias):
    center = tokens - lax.optimization_barrier(jnp.mean(tokens, axis=1, keepdims=True))
    spread = lax.optimization_barrier(jnp.mean(center * center, axis=1, keepdims=True))
    return center * lax.rsqrt(spread + epsilon) * ln_gain + ln_bias

def reference(tokens, ln_gain, ln_bias, weight_in, weight_out, expert_ids, combine_weights, owner_ids):
    normed = normalize(tokens, ln_gain, ln_bias).astype(jnp.bfloat16)
    flat_ids = expert_ids.reshape(N_DP, TOK_DEV * 2)
    one_hot = (flat_ids[:, :, None] == jnp.arange(EXPERTS, dtype=jnp.int32)[None, None, :]).astype(jnp.int32)
    slots = lax.optimization_barrier(jnp.sum((jnp.cumsum(one_hot, axis=1) - 1) * one_hot, axis=2)).astype(jnp.int32)
    blocks = jnp.arange(N_DP, dtype=jnp.int32)[:, None]
    target = ((flat_ids * N_DP + blocks) * CAP + slots).reshape(TOKENS * 2).astype(jnp.int32)
    rows = jnp.repeat(normed, 2, axis=0)
    buffer = jnp.zeros((EXPERTS * N_DP * CAP, D), jnp.bfloat16).at[target].set(rows)
    buffer = buffer.reshape(EXPERTS, N_DP * CAP, D)
    group = FF // N_EXPERT

    def expert(operands):
        inputs, first, second = operands
        pre = jnp.dot(inputs.astype(jnp.float32), first.astype(jnp.float32), precision=lax.Precision.HIGHEST)
        hidden = jax.nn.gelu(pre, approximate=True).astype(jnp.bfloat16)
        parts = jnp.einsum('rgf,gfd->rgd', hidden.reshape(-1, N_EXPERT, group).astype(jnp.float32), second.reshape(N_EXPERT, group, D).astype(jnp.float32), precision=lax.Precision.HIGHEST)
        rounded = lax.optimization_barrier(parts.astype(jnp.bfloat16))
        return lax.optimization_barrier(jnp.sum(rounded.astype(jnp.float32), axis=1))
    expert_out = lax.map(expert, (buffer, weight_in, weight_out))
    picked = expert_out.reshape(EXPERTS * N_DP * CAP, D)[target].reshape(TOKENS, 2, D)
    finished = tokens + lax.optimization_barrier(jnp.sum(combine_weights[:, :, None] * picked, axis=1))
    owners = owner_ids[:, 0]
    owner_hot = (owners[:, None] == jnp.arange(N_DP, dtype=jnp.int32)[None, :]).astype(jnp.int32)
    offsets = lax.optimization_barrier(jnp.sum((jnp.cumsum(owner_hot, axis=0) - 1) * owner_hot, axis=1)).astype(jnp.int32)
    row_base = (owners * OWN_IMG + offsets) * PATCH
    placed = (row_base[:, None] + jnp.arange(PATCH, dtype=jnp.int32)[None, :]).reshape(IMAGES * PATCH).astype(jnp.int32)
    delivered = jnp.zeros((N_DP * OWN_IMG * PATCH, D), jnp.float32).at[placed].set(finished)
    return delivered
```

```python
import functools

import jax
import jax.numpy as jnp
from jax import lax
from jax.experimental import pallas as pl
from jax.experimental.pallas import tpu as pltpu
from jax.sharding import PartitionSpec as P

PATCH = 256
CAP = 80
OWN_IMG = 4
CORES = 2


epsilon = 1e-06


def normalize(tokens, ln_gain, ln_bias):
    center = tokens - jnp.mean(tokens, axis=1, keepdims=True)
    spread = jnp.mean(center * center, axis=1, keepdims=True)
    return center * lax.rsqrt(spread + epsilon) * ln_gain + ln_bias


def general(tokens, ln_gain, ln_bias, weight_in, weight_out, expert_ids, combine_weights, owner_ids):
    groups = lax.axis_size("dp")
    columns = lax.axis_size("expert")
    tok_rows = tokens.shape[0]
    width = tokens.shape[1]
    share = width // columns
    local_experts = weight_in.shape[0]
    all_experts = local_experts * groups
    normed = normalize(tokens, ln_gain, ln_bias).astype(jnp.bfloat16)
    flat_ids = expert_ids.reshape(tok_rows * 2)
    one_hot = (flat_ids[:, None] == jnp.arange(all_experts, dtype=jnp.int32)[None, :]).astype(
        jnp.int32
    )
    slots = jnp.sum((jnp.cumsum(one_hot, axis=0) - 1) * one_hot, axis=1)
    target = flat_ids * CAP + slots
    outbound = (
        jnp.zeros((all_experts * CAP, width), jnp.bfloat16)
        .at[target]
        .set(jnp.repeat(normed, 2, axis=0))
    )
    outbound = outbound.reshape(groups, local_experts, CAP, width)
    pre = jnp.einsum(
        "sepd,edf->sepf",
        lax.all_to_all(outbound, "dp", split_axis=0, concat_axis=0, tiled=True),
        weight_in,
        preferred_element_type=jnp.float32,
    )
    hidden = jax.nn.gelu(pre, approximate=True).astype(jnp.bfloat16)
    moved = jnp.einsum(
        "sepf,efd->sepd", hidden, weight_out, preferred_element_type=jnp.float32
    ).astype(jnp.bfloat16)
    summed = lax.psum_scatter(
        moved.astype(jnp.float32).astype(jnp.bfloat16), "expert", scatter_dimension=3, tiled=True
    ).astype(jnp.float32)
    back = lax.all_to_all(summed, "dp", split_axis=0, concat_axis=0, tiled=True)
    picked = back.reshape(groups * local_experts * CAP, share)[target].reshape(tok_rows, 2, share)
    branch = jnp.sum(combine_weights[:, :, None] * picked, axis=1)
    base = lax.dynamic_slice_in_dim(tokens, lax.axis_index("expert") * share, share, 1)
    finished = base + branch
    img_dev = tok_rows // PATCH
    images = owner_ids.shape[0]
    owners = owner_ids[:, 0]
    position = jnp.arange(images, dtype=jnp.int32)
    source_dev = position // img_dev
    same_owner = owners[:, None] == owners[None, :]
    earlier = position[None, :] < position[:, None]
    offsets = jnp.sum((same_owner & earlier).astype(jnp.int32), axis=1)
    same_source = source_dev[:, None] == source_dev[None, :]
    local_rank = jnp.sum((same_owner & earlier & same_source).astype(jnp.int32), axis=1)
    device_row = lax.axis_index("dp")
    my_owners = lax.dynamic_slice_in_dim(owners, device_row * img_dev, img_dev)
    my_ranks = lax.dynamic_slice_in_dim(local_rank, device_row * img_dev, img_dev)
    sender_map = (
        jnp.arange(groups * img_dev, dtype=jnp.int32)[:, None]
        == (my_owners * img_dev + my_ranks)[None, :]
    ).astype(jnp.float32)
    outgoing = jnp.dot(
        sender_map, finished.reshape(img_dev, PATCH * share), precision=lax.Precision.HIGHEST
    )
    outgoing = outgoing.reshape(groups, img_dev, PATCH, share)
    arrived = lax.all_to_all(outgoing, "dp", split_axis=0, concat_axis=0, tiled=True)
    column_index = source_dev * img_dev + local_rank
    mine = (owners == device_row)[None, :]
    slot_pick = ((jnp.arange(OWN_IMG, dtype=jnp.int32)[:, None] == offsets[None, :]) & mine).astype(
        jnp.float32
    )
    column_pick = (
        column_index[:, None] == jnp.arange(groups * img_dev, dtype=jnp.int32)[None, :]
    ).astype(jnp.float32)
    placer = jnp.dot(slot_pick, column_pick, precision=lax.Precision.HIGHEST)
    delivered = jnp.dot(
        placer, arrived.reshape(groups * img_dev, PATCH * share), precision=lax.Precision.HIGHEST
    )
    return delivered.reshape(OWN_IMG * PATCH, share)


def whole(shape):
    return pl.BlockSpec(shape, lambda *_: (0,) * len(shape))


def dispatch_kernel(groups, locals_, meta, tok_ref, gain_ref, bias_ref, ids_ref, w_ref, out_ref, slot_ref, wtab_ref):
    y, core = meta[0], meta[1]
    experts = groups * locals_
    rows = tok_ref.shape[0]
    half = CAP // CORES
    ids = ids_ref[...]
    weights = w_ref[...]
    which = lax.broadcasted_iota(jnp.int32, (experts, rows), 0)
    first = which == ids[0:1, :]
    second = which == ids[1:2, :]
    named = first | second
    earlier = lax.broadcasted_iota(jnp.int32, (rows, rows), 0) < lax.broadcasted_iota(
        jnp.int32, (rows, rows), 1
    )
    before = jnp.dot(
        named.astype(jnp.float32).astype(jnp.bfloat16),
        earlier.astype(jnp.float32).astype(jnp.bfloat16),
        preferred_element_type=jnp.float32,
    )
    slot_ref[...] = jnp.where(named, before.astype(jnp.int32), -1)
    wtab_ref[...] = jnp.where(first, weights[0:1, :], 0.0) + jnp.where(second, weights[1:2, :], 0.0)
    tokens = tok_ref[...]
    normed = normalize(tokens, gain_ref[...], bias_ref[...]).astype(jnp.bfloat16)
    step = lax.broadcasted_iota(jnp.int32, (half, rows), 0) + core * half
    picks = []
    for g in range(groups):
        slots = slot_ref[pl.ds(g * locals_ + y, 1), :]
        picks.append((slots == step).astype(jnp.float32))
    pick = jnp.concatenate(picks, axis=0).astype(jnp.bfloat16)
    out_ref[...] = jnp.dot(pick, normed, preferred_element_type=jnp.float32).astype(jnp.bfloat16)


def dispatch(meta, tokens, gain, bias, ids, weights, groups, locals_):
    rows, width = tokens.shape
    experts = groups * locals_
    half = CAP // CORES
    return pl.pallas_call(
        functools.partial(dispatch_kernel, groups, locals_),
        out_shape=(
            jax.ShapeDtypeStruct((groups * half, width), jnp.bfloat16),
            jax.ShapeDtypeStruct((experts, rows), jnp.int32),
            jax.ShapeDtypeStruct((experts, rows), jnp.float32),
        ),
        grid_spec=pltpu.PrefetchScalarGridSpec(
            num_scalar_prefetch=1,
            grid=(1,),
            in_specs=[whole((rows, width)), whole((1, width)), whole((1, width)), whole((2, rows)), whole((2, rows))],
            out_specs=(whole((groups * half, width)), whole((experts, rows)), whole((experts, rows))),
        ),
        compiler_params=pltpu.CompilerParams(vmem_limit_bytes=48 << 20),
        cost_estimate=pl.CostEstimate(flops=2 * rows * width * groups * half, bytes_accessed=8 * rows * width, transcendentals=0),
        name="dispatch",
    )(meta, tokens, gain[None, :], bias[None, :], ids, weights)


def base_kernel(columns, meta, tok_ref, out_ref):
    share = tok_ref.shape[1] // columns
    for q in range(columns):

        @pl.when(meta[0] * CORES + meta[1] == q)
        def _():
            out_ref[...] = tok_ref[:, q * share : (q + 1) * share].T


def base_of(meta, tokens, columns):
    rows, width = tokens.shape
    share = width // columns
    return pl.pallas_call(
        functools.partial(base_kernel, columns),
        out_shape=jax.ShapeDtypeStruct((share, rows), jnp.float32),
        grid_spec=pltpu.PrefetchScalarGridSpec(
            num_scalar_prefetch=1,
            grid=(1,),
            in_specs=[whole((rows, width))],
            out_specs=whole((share, rows)),
        ),
        cost_estimate=pl.CostEstimate(flops=0, bytes_accessed=5 * rows * width, transcendentals=0),
        name="base",
    )(meta, tokens)


def expert_kernel(groups, columns, meta, xa_ref, xb_ref, first_ref, second_ref, keep_ref, send_ref, x_ref, acc_ref):
    y, core = meta[1], meta[2]
    half = CAP // CORES
    step, steps = pl.program_id(0), pl.num_programs(0)
    share = acc_ref.shape[1] // columns

    @pl.when(step == 0)
    def _():
        for g in range(groups):
            x_ref[(2 * g) * half : (2 * g + 1) * half, :] = xa_ref[g * half : (g + 1) * half, :]
            x_ref[(2 * g + 1) * half : (2 * g + 2) * half, :] = xb_ref[g * half : (g + 1) * half, :]

    pre = jnp.dot(x_ref[...], first_ref[0], preferred_element_type=jnp.float32)
    hidden = jax.nn.gelu(pre, approximate=True).astype(jnp.bfloat16)
    part = jnp.dot(hidden, second_ref[0], preferred_element_type=jnp.float32)

    @pl.when(step == 0)
    def _():
        acc_ref[...] = part

    @pl.when(step > 0)
    def _():
        acc_ref[...] += part

    @pl.when(step == steps - 1)
    def _():
        for q in range(columns):
            other = jnp.abs(q // CORES - y)
            mine = core == q % CORES

            @pl.when(mine)
            def _():
                keep_ref[other] = acc_ref[:, q * share : (q + 1) * share].astype(jnp.bfloat16)

            @pl.when(jnp.logical_not(mine))
            def _():
                for b in range(2 * groups):
                    send_ref[other, (b ^ 1) * half : (b ^ 1) * half + half, :] = acc_ref[
                        b * half : (b + 1) * half, q * share : (q + 1) * share
                    ].astype(jnp.bfloat16)


def expert(meta, xa, xb, weight_in, weight_out, groups, columns, name):
    width, units = weight_in.shape[1], weight_in.shape[2]
    rows = groups * CAP
    block = min(512, units)
    share = width // columns
    shape = jax.ShapeDtypeStruct((columns // CORES, rows, share), jnp.bfloat16)
    return pl.pallas_call(
        functools.partial(expert_kernel, groups, columns),
        out_shape=(shape, shape),
        grid_spec=pltpu.PrefetchScalarGridSpec(
            num_scalar_prefetch=1,
            grid=(units // block,),
            in_specs=[
                whole(xa.shape),
                whole(xb.shape),
                pl.BlockSpec((1, width, block), lambda f, m: (m[0], 0, f)),
                pl.BlockSpec((1, block, width), lambda f, m: (m[0], f, 0)),
            ],
            out_specs=(whole(shape.shape), whole(shape.shape)),
            scratch_shapes=[pltpu.VMEM((rows, width), jnp.bfloat16), pltpu.VMEM((rows, width), jnp.float32)],
        ),
        compiler_params=pltpu.CompilerParams(vmem_limit_bytes=56 << 20),
        cost_estimate=pl.CostEstimate(flops=4 * rows * width * units, bytes_accessed=4 * width * units + 4 * rows * width, transcendentals=rows * units),
        name=name,
    )(meta, xa, xb, weight_in, weight_out)


def combine_kernel(groups, locals_, relative, meta, back_ref, slot_ref, wtab_ref, base_ref, out_ref):
    y, core = meta[0], meta[1]
    half = CAP // CORES
    rows = slot_ref.shape[1]
    step = lax.broadcasted_iota(jnp.int32, (half, rows), 0)
    which = y if relative == 0 else 1 - y
    blocks = []
    for g in range(groups):
        slots = slot_ref[pl.ds(g * locals_ + which, 1), :]
        weights = wtab_ref[pl.ds(g * locals_ + which, 1), :]
        for h in range(CORES):
            at = core if h == 0 else 1 - core
            blocks.append(jnp.where(slots == step + at * half, weights, 0.0))
    matrix = jnp.concatenate(blocks, axis=0)
    high = matrix.astype(jnp.bfloat16)
    low = (matrix - high.astype(jnp.float32)).astype(jnp.bfloat16)
    back = back_ref[...]
    turned = (((0,), (0,)), ((), ()))
    total = base_ref[...] + lax.dot_general(back, high, turned, preferred_element_type=jnp.float32)
    total = total + lax.dot_general(back, low, turned, preferred_element_type=jnp.float32)
    out_ref[...] = total.astype(out_ref.dtype)


def combine(meta, back, slots, wtab, base, groups, locals_, relative, dtype):
    share, rows = base.shape
    return pl.pallas_call(
        functools.partial(combine_kernel, groups, locals_, relative),
        out_shape=jax.ShapeDtypeStruct((share, rows), dtype),
        grid_spec=pltpu.PrefetchScalarGridSpec(
            num_scalar_prefetch=1,
            grid=(1,),
            in_specs=[whole(back.shape), whole(slots.shape), whole(wtab.shape), whole(base.shape)],
            out_specs=whole((share, rows)),
        ),
        compiler_params=pltpu.CompilerParams(vmem_limit_bytes=48 << 20),
        cost_estimate=pl.CostEstimate(flops=4 * share * rows * groups * CAP, bytes_accessed=2 * back.size + 8 * share * rows, transcendentals=0),
        name="combine%d" % relative,
    )(meta, back, slots, wtab, base)


def place(ring, groups, me):
    return jnp.where(me % 2 == 0, me // 2, groups - 1 - me // 2)


def unplace(groups, position):
    return jnp.where(position < groups // 2, 2 * position, 2 * (groups - 1 - position) + 1)


def deliver_kernel(groups, img_dev, deltas, meta, owners, *refs):
    blocks, out_ref, stage, sems = refs[: len(deltas)], refs[-3], refs[-2], refs[-1]
    me = meta[2]
    images = groups * img_dev
    share = out_ref.shape[0]

    def each(act):
        for number, (delta, low) in enumerate(deltas):
            position = lax.rem(place(None, groups, me) + delta + groups, groups)
            device = unplace(groups, position)
            height = blocks[number].shape[0]
            for h in range(img_dev):
                image = device * img_dev + h
                offset = jnp.int32(0)
                for j in range(images):
                    offset += jnp.where((j < image) & (owners[j] == me), 1, 0)

                @pl.when(owners[image] == me)
                def _():
                    copy = pltpu.make_async_copy(
                        blocks[number].at[:, h * PATCH : (h + 1) * PATCH],
                        stage.at[offset, low : low + height, :],
                        sems.at[number, h],
                    )
                    act(copy)

    each(lambda copy: copy.start())
    each(lambda copy: copy.wait())
    count = jnp.int32(0)
    for j in range(images):
        count += jnp.where(owners[j] == me, 1, 0)
    for s in range(OWN_IMG):

        @pl.when(s < count)
        def _():
            out_ref[:, s * PATCH : (s + 1) * PATCH] = stage[s].astype(jnp.float32)

        @pl.when(s >= count)
        def _():
            out_ref[:, s * PATCH : (s + 1) * PATCH] = jnp.zeros((share, PATCH), jnp.float32)


def deliver(meta, owners, blocks, deltas, groups, img_dev, share):
    return pl.pallas_call(
        functools.partial(deliver_kernel, groups, img_dev, deltas),
        out_shape=jax.ShapeDtypeStruct((share, OWN_IMG * PATCH), jnp.float32),
        grid_spec=pltpu.PrefetchScalarGridSpec(
            num_scalar_prefetch=2,
            grid=(1,),
            in_specs=[pl.BlockSpec(memory_space=pl.ANY)] * len(blocks),
            out_specs=whole((share, OWN_IMG * PATCH)),
            scratch_shapes=[
                pltpu.VMEM((OWN_IMG, share, PATCH), jnp.bfloat16),
                pltpu.SemaphoreType.DMA((len(blocks), img_dev)),
            ],
        ),
        compiler_params=pltpu.CompilerParams(vmem_limit_bytes=32 << 20),
        name="deliver",
    )(meta, owners, *blocks)


def swap(x, columns, distance):
    return lax.ppermute(x, "expert", [(i, i ^ distance) for i in range(columns)])


def fast(tokens, ln_gain, ln_bias, weight_in, weight_out, expert_ids, combine_weights, owner_ids):
    groups = lax.axis_size("dp")
    columns = lax.axis_size("expert")
    rows, width = tokens.shape
    share = width // columns
    locals_ = weight_in.shape[0]
    half = CAP // CORES
    col = lax.axis_index("expert")
    me = lax.axis_index("dp")
    y, core = col // CORES, col % CORES
    meta = jnp.stack([y, core, me]).astype(jnp.int32)
    sent, slots, wtab = dispatch(meta, tokens, ln_gain, ln_bias, expert_ids.T, combine_weights.T, groups, locals_)
    mine = lax.all_to_all(sent.reshape(groups, half, width), "dp", split_axis=0, concat_axis=0, tiled=True)
    mine = mine.reshape(groups * half, width)
    theirs = swap(mine, columns, CORES)
    mine_other = swap(mine, columns, 1)
    base = base_of(meta, tokens, columns)
    meta1 = jnp.stack([y, y, core]).astype(jnp.int32)
    meta2 = jnp.stack([1 - y, y, core]).astype(jnp.int32)
    keep1, send1 = expert(meta1, mine, mine_other, weight_in, weight_out, groups, columns, "first")
    recv1 = swap(send1, columns, 1)
    theirs_other = swap(theirs, columns, 1)
    across1 = swap(keep1[1] + recv1[1], columns, CORES)
    own1 = keep1[0] + recv1[0]
    keep2, send2 = expert(meta2, theirs, theirs_other, weight_in, weight_out, groups, columns, "second")
    recv2 = swap(send2, columns, 1)
    across2 = swap(keep2[1] + recv2[1], columns, CORES)
    total2 = keep2[0] + recv2[0] + across1

    def back(total):
        got = lax.all_to_all(total.reshape(groups, CAP, share), "dp", split_axis=0, concat_axis=0, tiled=True)
        return got.reshape(groups * CAP, share)

    part = combine(meta, back(total2), slots, wtab, base, groups, locals_, 1, jnp.float32)
    total1 = own1 + across2
    finished = combine(meta, back(total1), slots, wtab, part, groups, locals_, 0, jnp.bfloat16)

    order = [2 * i for i in range(groups // 2)] + [2 * i + 1 for i in reversed(range(groups // 2))]
    ahead = [(order[i], order[(i + 1) % groups]) for i in range(groups)]
    behind = [(b, a) for a, b in ahead]
    blocks, deltas = [finished], [(0, 0)]
    up = down = finished
    for s in range(1, groups // 2):
        up, down = lax.ppermute(up, "dp", ahead), lax.ppermute(down, "dp", behind)
        blocks += [up, down]
        deltas += [(-s, 0), (s, 0)]
    cut = share // 2
    blocks += [lax.ppermute(up[:cut], "dp", ahead), lax.ppermute(down[cut:], "dp", behind)]
    deltas += [(-(groups // 2), 0), (groups // 2, cut)]
    img_dev = rows // PATCH
    result = deliver(meta, owner_ids[:, 0], blocks, tuple(deltas), groups, img_dev, share)
    return result.T


def solution(mesh):
    small = mesh.shape["expert"] == 2 * CORES and mesh.shape["dp"] % 2 == 0
    return jax.shard_map(
        fast if small else general,
        mesh=mesh,
        in_specs=(
            P("dp", None),
            P(),
            P(),
            P("dp", None, "expert"),
            P("dp", "expert", None),
            P("dp", None),
            P("dp", None),
            P(),
        ),
        out_specs=P("dp", "expert"),
        check_vma=False,
    )
```

```python
import functools

import jax
import jax.numpy as jnp
from jax import lax
from jax.experimental import pallas as pl
from jax.experimental.pallas import tpu as pltpu
from jax.sharding import PartitionSpec as P


PATCH = 256
CAP = 80
OWN_IMG = 4
CORES = 2


epsilon = 1e-06


def normalize(tokens, ln_gain, ln_bias):
    center = tokens - jnp.mean(tokens, axis=1, keepdims=True)
    spread = jnp.mean(center * center, axis=1, keepdims=True)
    return center * lax.rsqrt(spread + epsilon) * ln_gain + ln_bias


def general(tokens, ln_gain, ln_bias, weight_in, weight_out, expert_ids, combine_weights, owner_ids):
    groups = lax.axis_size("dp")
    columns = lax.axis_size("expert")
    tok_rows = tokens.shape[0]
    width = tokens.shape[1]
    share = width // columns
    local_experts = weight_in.shape[0]
    all_experts = local_experts * groups
    normed = normalize(tokens, ln_gain, ln_bias).astype(jnp.bfloat16)
    flat_ids = expert_ids.reshape(tok_rows * 2)
    one_hot = (flat_ids[:, None] == jnp.arange(all_experts, dtype=jnp.int32)[None, :]).astype(
        jnp.int32
    )
    slots = jnp.sum((jnp.cumsum(one_hot, axis=0) - 1) * one_hot, axis=1)
    target = flat_ids * CAP + slots
    outbound = (
        jnp.zeros((all_experts * CAP, width), jnp.bfloat16)
        .at[target]
        .set(jnp.repeat(normed, 2, axis=0))
    )
    outbound = outbound.reshape(groups, local_experts, CAP, width)
    pre = jnp.einsum(
        "sepd,edf->sepf",
        lax.all_to_all(outbound, "dp", split_axis=0, concat_axis=0, tiled=True),
        weight_in,
        preferred_element_type=jnp.float32,
    )
    hidden = jax.nn.gelu(pre, approximate=True).astype(jnp.bfloat16)
    moved = jnp.einsum(
        "sepf,efd->sepd", hidden, weight_out, preferred_element_type=jnp.float32
    ).astype(jnp.bfloat16)
    summed = lax.psum_scatter(
        moved.astype(jnp.float32).astype(jnp.bfloat16), "expert", scatter_dimension=3, tiled=True
    ).astype(jnp.float32)
    back = lax.all_to_all(summed, "dp", split_axis=0, concat_axis=0, tiled=True)
    picked = back.reshape(groups * local_experts * CAP, share)[target].reshape(tok_rows, 2, share)
    branch = jnp.sum(combine_weights[:, :, None] * picked, axis=1)
    base = lax.dynamic_slice_in_dim(tokens, lax.axis_index("expert") * share, share, 1)
    finished = base + branch
    img_dev = tok_rows // PATCH
    images = owner_ids.shape[0]
    owners = owner_ids[:, 0]
    position = jnp.arange(images, dtype=jnp.int32)
    source_dev = position // img_dev
    same_owner = owners[:, None] == owners[None, :]
    earlier = position[None, :] < position[:, None]
    offsets = jnp.sum((same_owner & earlier).astype(jnp.int32), axis=1)
    same_source = source_dev[:, None] == source_dev[None, :]
    local_rank = jnp.sum((same_owner & earlier & same_source).astype(jnp.int32), axis=1)
    device_row = lax.axis_index("dp")
    my_owners = lax.dynamic_slice_in_dim(owners, device_row * img_dev, img_dev)
    my_ranks = lax.dynamic_slice_in_dim(local_rank, device_row * img_dev, img_dev)
    sender_map = (
        jnp.arange(groups * img_dev, dtype=jnp.int32)[:, None]
        == (my_owners * img_dev + my_ranks)[None, :]
    ).astype(jnp.float32)
    outgoing = jnp.dot(
        sender_map, finished.reshape(img_dev, PATCH * share), precision=lax.Precision.HIGHEST
    )
    outgoing = outgoing.reshape(groups, img_dev, PATCH, share)
    arrived = lax.all_to_all(outgoing, "dp", split_axis=0, concat_axis=0, tiled=True)
    column_index = source_dev * img_dev + local_rank
    mine = (owners == device_row)[None, :]
    slot_pick = ((jnp.arange(OWN_IMG, dtype=jnp.int32)[:, None] == offsets[None, :]) & mine).astype(
        jnp.float32
    )
    column_pick = (
        column_index[:, None] == jnp.arange(groups * img_dev, dtype=jnp.int32)[None, :]
    ).astype(jnp.float32)
    placer = jnp.dot(slot_pick, column_pick, precision=lax.Precision.HIGHEST)
    delivered = jnp.dot(
        placer, arrived.reshape(groups * img_dev, PATCH * share), precision=lax.Precision.HIGHEST
    )
    return delivered.reshape(OWN_IMG * PATCH, share)


PIECE = 40
PACKED = 136


def whole(shape):
    return pl.BlockSpec(shape, lambda *_: (0,) * len(shape))


def params(mib):
    return pltpu.CompilerParams(vmem_limit_bytes=mib << 20)


def dispatch_kernel(groups, locals_, meta, tok_ref, gain_ref, bias_ref, ids_ref, w_ref, slot_ref, wtab_ref, *out_refs):
    y, core, me = meta[0], meta[1], meta[2]
    experts = groups * locals_
    rows = tok_ref.shape[0]
    ids = ids_ref[...]
    weights = w_ref[...]
    which = lax.broadcasted_iota(jnp.int32, (experts, rows), 0)
    first = which == ids[0:1, :]
    second = which == ids[1:2, :]
    named = first | second
    earlier = lax.broadcasted_iota(jnp.int32, (rows, rows), 0) < lax.broadcasted_iota(
        jnp.int32, (rows, rows), 1
    )
    before = jnp.dot(
        named.astype(jnp.float32).astype(jnp.bfloat16),
        earlier.astype(jnp.float32).astype(jnp.bfloat16),
        preferred_element_type=jnp.float32,
    )
    slot_ref[...] = jnp.where(named, before.astype(jnp.int32), -1)
    wtab_ref[...] = jnp.where(first, weights[0:1, :], 0.0) + jnp.where(second, weights[1:2, :], 0.0)
    normed = normalize(tok_ref[...], gain_ref[...], bias_ref[...]).astype(jnp.bfloat16)
    step = lax.broadcasted_iota(jnp.int32, (PIECE, rows), 0) + core * PIECE
    picks = []
    for s in range(groups):
        slots = slot_ref[pl.ds((me ^ s) * locals_ + y, 1), :]
        picks.append((slots == step).astype(jnp.float32))
    pick = jnp.concatenate(picks, axis=0).astype(jnp.bfloat16)
    sent = jnp.dot(pick, normed, preferred_element_type=jnp.float32).astype(jnp.bfloat16)
    for s in range(groups):
        out_refs[s][...] = sent[s * PIECE : (s + 1) * PIECE, :]


def dispatch(meta, tokens, gain, bias, ids, weights, groups, locals_):
    rows, width = tokens.shape
    experts = groups * locals_
    return pl.pallas_call(
        functools.partial(dispatch_kernel, groups, locals_),
        out_shape=(
            jax.ShapeDtypeStruct((experts, rows), jnp.int32),
            jax.ShapeDtypeStruct((experts, rows), jnp.float32),
        )
        + (jax.ShapeDtypeStruct((PIECE, width), jnp.bfloat16),) * groups,
        grid_spec=pltpu.PrefetchScalarGridSpec(
            num_scalar_prefetch=1,
            grid=(1,),
            in_specs=[whole((rows, width)), whole((1, width)), whole((1, width)), whole((2, rows)), whole((2, rows))],
            out_specs=(whole((experts, rows)),) * 2 + (whole((PIECE, width)),) * groups,
        ),
        compiler_params=params(63),
        cost_estimate=pl.CostEstimate(flops=2 * rows * width * groups * PIECE, bytes_accessed=8 * rows * width, transcendentals=0),
        name="dispatch",
    )(meta, tokens, gain[None, :], bias[None, :], ids, weights)


def base_kernel(columns, meta, tok_ref, out_ref):
    share = tok_ref.shape[1] // columns
    for q in range(columns):

        @pl.when(meta[0] * CORES + meta[1] == q)
        def _():
            out_ref[...] = tok_ref[:, q * share : (q + 1) * share].T


def base_of(meta, tokens, columns):
    rows, width = tokens.shape
    share = width // columns
    return pl.pallas_call(
        functools.partial(base_kernel, columns),
        out_shape=jax.ShapeDtypeStruct((share, rows), jnp.float32),
        grid_spec=pltpu.PrefetchScalarGridSpec(
            num_scalar_prefetch=1,
            grid=(1,),
            in_specs=[whole((rows, width))],
            out_specs=whole((share, rows)),
        ),
        compiler_params=params(16),
        cost_estimate=pl.CostEstimate(flops=0, bytes_accessed=5 * rows * width, transcendentals=0),
        name="base",
    )(meta, tokens)


def pack(ref, at, block):
    full = block.shape[1] // 128
    for j in range(full):
        ref[at + (slice(j * PIECE, (j + 1) * PIECE),)] = block[:, j * 128 : (j + 1) * 128]
    rest = block[:, full * 128 :]
    empty = jnp.zeros((8, rest.shape[1]), rest.dtype)
    third = jnp.concatenate([rest[32:40], empty], axis=0)
    last = jnp.concatenate([empty, empty], axis=0)
    ref[at + (slice(full * PIECE, PACKED),)] = jnp.concatenate([rest[0:16], rest[16:32], third, last], axis=1)


def unpack(block, share):
    full = share // 128
    wide = share - full * 128
    rest = block[full * PIECE : PACKED, :]
    rest = jnp.concatenate([rest[:, 0:wide], rest[:, wide : 2 * wide], rest[0:8, 2 * wide : 3 * wide]], axis=0)
    return jnp.concatenate([block[j * PIECE : (j + 1) * PIECE] for j in range(full)] + [rest], axis=1)


def expert_kernel(groups, columns, meta, xan_ref, xbn_ref, xaf_ref, xbf_ref, first_ref, second_ref, own_ref, across_ref, send_ref, acc_ref, stage_ref):
    y, core = meta[1], meta[2]
    step = pl.program_id(0)
    share = acc_ref.shape[2] // columns
    near = groups // 2

    def part(x_ref):
        pre = jnp.dot(x_ref[...], first_ref[0], preferred_element_type=jnp.float32)
        hidden = jax.nn.gelu(pre, approximate=True).astype(jnp.bfloat16)
        return jnp.dot(hidden, second_ref[0], preferred_element_type=jnp.float32)

    inputs = (xan_ref, xbn_ref, xaf_ref, xbf_ref)

    @pl.when(step == 0)
    def _():
        for i, x_ref in enumerate(inputs):
            acc_ref[i] = part(x_ref)

    @pl.when(step == 1)
    def _():
        for i, x_ref in enumerate(inputs):
            half = core if i % 2 == 0 else 1 - core
            total = (acc_ref[i] + part(x_ref)).astype(jnp.bfloat16)
            for q in range(columns):
                for t in range(near):
                    block = total[t * PIECE : (t + 1) * PIECE, q * share : (q + 1) * share]
                    pack(stage_ref, (q, (i // 2) * near + t, half), block)
        here, there = y * CORES, (1 - y) * CORES
        own_ref[...] = stage_ref[here + core]
        across_ref[...] = stage_ref[there + core]
        send_ref[0] = stage_ref[here + 1 - core]
        send_ref[1] = stage_ref[there + 1 - core]


def expert(meta, inputs, weight_in, weight_out, groups, columns):
    width, units = weight_in.shape[1], weight_in.shape[2]
    rows = groups * CAP
    block = units // 2
    shape = jax.ShapeDtypeStruct((groups, CORES, PACKED, 128), jnp.bfloat16)
    pair = jax.ShapeDtypeStruct((2,) + shape.shape, jnp.bfloat16)
    return pl.pallas_call(
        functools.partial(expert_kernel, groups, columns),
        out_shape=(shape, shape, pair),
        grid_spec=pltpu.PrefetchScalarGridSpec(
            num_scalar_prefetch=1,
            grid=(2,),
            in_specs=[whole(x.shape) for x in inputs]
            + [
                pl.BlockSpec((1, width, block), lambda f, m: (m[0], 0, f)),
                pl.BlockSpec((1, block, width), lambda f, m: (m[0], f, 0)),
            ],
            out_specs=(whole(shape.shape), whole(shape.shape), whole(pair.shape)),
            scratch_shapes=[
                pltpu.VMEM((4, rows // 4, width), jnp.float32),
                pltpu.VMEM((columns,) + shape.shape, jnp.bfloat16),
            ],
        ),
        compiler_params=params(40),
        cost_estimate=pl.CostEstimate(flops=4 * rows * width * units, bytes_accessed=4 * width * units + 4 * rows * width, transcendentals=rows * units),
    )(meta, *inputs, weight_in, weight_out)


def last_kernel(own_ref, over_ref, recv_ref, came_ref, send_ref, *out_refs):
    send_ref[...] = over_ref[...] + recv_ref[1]
    for s, out_ref in enumerate(out_refs):
        out_ref[...] = own_ref[s] + recv_ref[0, s] + came_ref[s]


def last(own, over, recv, came):
    blocks = (jax.ShapeDtypeStruct(own.shape[1:], own.dtype),) * own.shape[0]
    return pl.pallas_call(
        last_kernel,
        out_shape=(jax.ShapeDtypeStruct(own.shape, own.dtype),) + blocks,
        grid=(1,),
        in_specs=[whole(own.shape), whole(over.shape), whole(recv.shape), whole(came.shape)],
        out_specs=(whole(own.shape),) + (whole(own.shape[1:]),) * own.shape[0],
        compiler_params=params(16),
        cost_estimate=pl.CostEstimate(flops=3 * own.size, bytes_accessed=12 * own.size, transcendentals=0),
        name="last",
    )(own, over, recv, came)


def join_kernel(own_ref, came_ref, *out_refs):
    for s, out_ref in enumerate(out_refs):
        out_ref[...] = own_ref[s] + came_ref[s]


def join(own, came):
    blocks = (jax.ShapeDtypeStruct(own.shape[1:], own.dtype),) * own.shape[0]
    return pl.pallas_call(
        join_kernel,
        out_shape=blocks,
        grid=(1,),
        in_specs=[whole(own.shape), whole(came.shape)],
        out_specs=(whole(own.shape[1:]),) * own.shape[0],
        compiler_params=params(16),
        cost_estimate=pl.CostEstimate(flops=own.size, bytes_accessed=6 * own.size, transcendentals=0),
        name="join",
    )(own, came)


def combine_kernel(groups, locals_, relative, meta, slot_ref, wtab_ref, base_ref, *refs):
    back_refs, out_ref = refs[:-1], refs[-1]
    y, me = meta[0], meta[2]
    share, rows = base_ref.shape
    step = lax.broadcasted_iota(jnp.int32, (PIECE, rows), 0)
    which = y if relative == 0 else 1 - y
    blocks, backs = [], []
    for s in range(groups):
        slots = slot_ref[pl.ds((me ^ s) * locals_ + which, 1), :]
        weights = wtab_ref[pl.ds((me ^ s) * locals_ + which, 1), :]
        for h in range(CORES):
            blocks.append(jnp.where(slots == step + h * PIECE, weights, 0.0))
            backs.append(unpack(back_refs[s][h], share))
    matrix = jnp.concatenate(blocks, axis=0)
    high = matrix.astype(jnp.bfloat16)
    low = (matrix - high.astype(jnp.float32)).astype(jnp.bfloat16)
    back = jnp.concatenate(backs, axis=0)
    turned = (((0,), (0,)), ((), ()))
    total = base_ref[...] + lax.dot_general(back, high, turned, preferred_element_type=jnp.float32)
    total = total + lax.dot_general(back, low, turned, preferred_element_type=jnp.float32)
    out_ref[...] = total.astype(out_ref.dtype)


def combine(meta, backs, slots, wtab, base, groups, locals_, relative, dtype):
    share, rows = base.shape
    return pl.pallas_call(
        functools.partial(combine_kernel, groups, locals_, relative),
        out_shape=jax.ShapeDtypeStruct((share, rows), dtype),
        grid_spec=pltpu.PrefetchScalarGridSpec(
            num_scalar_prefetch=1,
            grid=(1,),
            in_specs=[whole(slots.shape), whole(wtab.shape), whole(base.shape)] + [whole(b.shape) for b in backs],
            out_specs=whole((share, rows)),
        ),
        compiler_params=params(24),
        cost_estimate=pl.CostEstimate(flops=4 * share * rows * groups * CAP, bytes_accessed=2 * share * groups * CAP + 8 * share * rows, transcendentals=0),
    )(meta, slots, wtab, base, *backs)


def place(groups, me):
    return jnp.where(me % 2 == 0, me // 2, groups - 1 - me // 2)


def unplace(groups, position):
    return jnp.where(position < groups // 2, 2 * position, 2 * (groups - 1 - position) + 1)


def deliver_kernel(groups, img_dev, deltas, meta, owners, *refs):
    blocks, out_ref, stage, sems = refs[: len(deltas)], refs[-3], refs[-2], refs[-1]
    me = meta[2]
    images = groups * img_dev
    share = out_ref.shape[0]

    def each(act):
        for number, (delta, low) in enumerate(deltas):
            position = lax.rem(place(groups, me) + delta + groups, groups)
            device = unplace(groups, position)
            height = blocks[number].shape[0]
            for h in range(img_dev):
                image = device * img_dev + h
                offset = jnp.int32(0)
                for j in range(images):
                    offset += jnp.where((j < image) & (owners[j] == me), 1, 0)

                @pl.when(owners[image] == me)
                def _():
                    copy = pltpu.make_async_copy(
                        blocks[number].at[:, h * PATCH : (h + 1) * PATCH],
                        stage.at[offset, low : low + height, :],
                        sems.at[number, h],
                    )
                    act(copy)

    each(lambda copy: copy.start())
    each(lambda copy: copy.wait())
    count = jnp.int32(0)
    for j in range(images):
        count += jnp.where(owners[j] == me, 1, 0)
    for s in range(OWN_IMG):

        @pl.when(s < count)
        def _():
            out_ref[:, s * PATCH : (s + 1) * PATCH] = stage[s].astype(jnp.float32)

        @pl.when(s >= count)
        def _():
            out_ref[:, s * PATCH : (s + 1) * PATCH] = jnp.zeros((share, PATCH), jnp.float32)


def deliver(meta, owners, blocks, deltas, groups, img_dev, share):
    return pl.pallas_call(
        functools.partial(deliver_kernel, groups, img_dev, deltas),
        out_shape=jax.ShapeDtypeStruct((share, OWN_IMG * PATCH), jnp.float32),
        grid_spec=pltpu.PrefetchScalarGridSpec(
            num_scalar_prefetch=2,
            grid=(1,),
            in_specs=[pl.BlockSpec(memory_space=pl.ANY)] * len(blocks),
            out_specs=whole((share, OWN_IMG * PATCH)),
            scratch_shapes=[
                pltpu.VMEM((OWN_IMG, share, PATCH), jnp.bfloat16),
                pltpu.SemaphoreType.DMA((len(blocks), img_dev)),
            ],
        ),
        compiler_params=pltpu.CompilerParams(vmem_limit_bytes=32 << 20),
        name="deliver",
    )(meta, owners, *blocks)


def swap(x, columns, distance):
    return lax.ppermute(x, "expert", [(i, i ^ distance) for i in range(columns)])


def over(x, groups, distance):
    return lax.ppermute(x, "dp", [(i, i ^ distance) for i in range(groups)])


def fast_body(tokens, ln_gain, ln_bias, weight_in, weight_out, expert_ids, combine_weights, owner_ids):
    groups = lax.axis_size("dp")
    columns = lax.axis_size("expert")
    rows, width = tokens.shape
    share = width // columns
    locals_ = weight_in.shape[0]
    col = lax.axis_index("expert")
    me = lax.axis_index("dp")
    y, core = col // CORES, col % CORES
    near = groups // 2
    meta = jnp.stack([y, core, me]).astype(jnp.int32)
    slots, wtab, *sent = dispatch(meta, tokens, ln_gain, ln_bias, expert_ids.T, combine_weights.T, groups, locals_)
    got = [sent[0]] + [over(sent[s], groups, s) for s in range(1, groups)]
    an = jnp.concatenate(got[:near], axis=0)
    af = jnp.concatenate(got[near:], axis=0)
    yan = swap(an, columns, CORES)
    yaf = swap(af, columns, CORES)
    bn, bf = swap(an, columns, 1), swap(af, columns, 1)
    base = base_of(meta, tokens, columns)
    meta1 = jnp.stack([y, y, core]).astype(jnp.int32)
    meta2 = jnp.stack([1 - y, y, core]).astype(jnp.int32)
    own1, over1, send1 = expert(meta1, (an, bn, af, bf), weight_in, weight_out, groups, columns)
    yaf, own1, over1, send1 = lax.optimization_barrier((yaf, own1, over1, send1))
    recv1 = swap(send1, columns, 1)
    ybn, ybf = swap(yan, columns, 1), swap(yaf, columns, 1)
    out1 = over1 + recv1[1]
    own1 = own1 + recv1[0]
    out1, own1, yan, ybn, yaf, ybf = lax.optimization_barrier((out1, own1, yan, ybn, yaf, ybf))
    came1 = swap(out1, columns, CORES)
    own2, over2, send2 = expert(meta2, (yan, ybn, yaf, ybf), weight_in, weight_out, groups, columns)
    recv2 = swap(send2, columns, 1)
    out2, *total2 = last(own2, over2, recv2, came1)
    came2 = swap(out2, columns, CORES)
    back2 = [total2[0]] + [over(total2[s], groups, s) for s in range(1, groups)]
    total1 = join(own1, came2)
    back1 = [total1[0]] + [over(total1[s], groups, s) for s in range(1, groups)]
    part = combine(meta, back2, slots, wtab, base, groups, locals_, 1, jnp.float32)
    finished = combine(meta, back1, slots, wtab, part, groups, locals_, 0, jnp.bfloat16)

    order = [2 * i for i in range(groups // 2)] + [2 * i + 1 for i in reversed(range(groups // 2))]
    ahead = [(order[i], order[(i + 1) % groups]) for i in range(groups)]
    behind = [(b, a) for a, b in ahead]
    blocks, deltas = [finished], [(0, 0)]
    up = down = finished
    for s in range(1, groups // 2):
        up, down = lax.ppermute(up, "dp", ahead), lax.ppermute(down, "dp", behind)
        blocks += [up, down]
        deltas += [(-s, 0), (s, 0)]
    cut = share // 2
    blocks += [lax.ppermute(up[:cut], "dp", ahead), lax.ppermute(down[cut:], "dp", behind)]
    deltas += [(-(groups // 2), 0), (groups // 2, cut)]
    img_dev = rows // PATCH
    result = deliver(meta, owner_ids[:, 0], blocks, tuple(deltas), groups, img_dev, share)
    return result.T


def fast(*arrays):
    return fast_body(*arrays)


def solution(mesh):
    dp = mesh.shape["dp"]
    small = mesh.shape["expert"] == 2 * CORES and dp >= 4 and dp & (dp - 1) == 0
    return jax.shard_map(
        fast if small else general,
        mesh=mesh,
        in_specs=(
            P("dp", None),
            P(),
            P(),
            P("dp", None, "expert"),
            P("dp", "expert", None),
            P("dp", None),
            P("dp", None),
            P(),
        ),
        out_specs=P("dp", "expert"),
        check_vma=False,
    )
```
